32 devices in a mesh: grp: 2 (over x), sp: 16 (over z, y, core).
Axes of the slice: x: 2, y: 2, z: 4, core: 2. Of those that a mesh axis runs over, the one named last changes fastest.
Arguments:
- volume: bfloat16 [64, 32, 48, 256], P(('grp', 'sp')), parts along dimension 0, may hold values from -8 to 8
- norm_gain: float32 [256], replicated, may hold values from 0.5 to 1.5
- norm_bias: float32 [256], replicated, may hold values from -3 to 3
- conv_weight: bfloat16 [27, 256, 256], replicated, may hold values from -0.078125 to 0.078125
- down_weight: bfloat16 [8, 256, 512], replicated, may hold values from -0.125 to 0.125
Outputs:
- reduced: bfloat16 [32, 16, 24, 512], P(('grp', 'sp')), parts along dimension 0
The draws below stay inside these ranges and needn't reach their ends.
There are 2 independent parts, one for each index of `grp`. The reference program is written for one: setup_inputs(seed, part) draws one part's arguments, and reference() takes and returns one part's arrays. A program takes and returns all parts, laid end to end along the dimension named above; an argument that names none is the same for every part. Nothing has to cross between parts.
All inputs are finite; a program needn't handle non-finite values.
Results may differ from the reference program's by a relative error of at most 0.0058.
Values may be sent and summed in bfloat16 or wider, within the bound.
A program may use at most 192 MiB of HBM per device.

```python
import jax
import jax.numpy as jnp
from jax import lax

C = 256
C2 = 512
GROUPS = 32
HH = 32
WW = 48
DEPTH = 32


def draw_volume(key, part):
    key_noise = jax.random.fold_in(key, 11)
    key_chan = jax.random.fold_in(key, 12)
    depth_pos = jnp.arange(DEPTH, dtype=jnp.float32) / max(DEPTH - 1, 1)
    plane = (1.0 + 2.0 * depth_pos)[:, None, None, None]
    channel = jnp.exp(jax.random.uniform(key_chan, (C,), jnp.float32, -1.15, 1.15))
    noise = jax.random.normal(key_noise, (DEPTH, HH, WW, C), jnp.float32)
    values = noise * channel * plane
    return jnp.clip(values, -8.0, 8.0).astype(jnp.bfloat16)


def normal_values(rng, shape, scale, reach, kind=jnp.bfloat16):
    drawn = scale * jax.random.normal(rng, shape, jnp.float32)
    return jnp.clip(drawn, min=-reach, max=reach).astype(kind)


def setup_inputs(seed: int = 0, part: int = 0) -> dict:
    splits = jax.random.split(jax.random.key(seed), 6)
    part_splits = jax.random.split(jax.random.fold_in(splits[5], part), 6)
    return {
        "volume": draw_volume(jax.random.fold_in(jax.random.fold_in(splits[5], part), 71), part),
        "norm_gain": jnp.clip(1.0 + 0.1 * jax.random.normal(splits[1], (C,), jnp.float32), 0.5, 1.5),
        "norm_bias": normal_values(splits[2], (C,), 0.5, 3.0, jnp.float32),
        "conv_weight": normal_values(splits[3], (27, C, C), (27 * C) ** -0.5, 0.078125),
        "down_weight": normal_values(splits[4], (8, C, C2), (8 * C) ** -0.5, 0.125),
    }


def reference(volume, norm_gain, norm_bias, conv_weight, down_weight):
    source = volume.astype(jnp.float32)
    per_group = C // GROUPS
    grouped = source.reshape(DEPTH, HH, WW, GROUPS, per_group)
    count = DEPTH * HH * WW * per_group
    total = lax.optimization_barrier(jnp.sum(grouped, axis=(0, 1, 2, 4)))
    squares = lax.optimization_barrier(jnp.sum(grouped * grouped, axis=(0, 1, 2, 4)))
    mean = total / count
    var = squares / count - mean * mean
    inv = 1.0 / jnp.sqrt(var + 1e-05)
    scale = norm_gain * jnp.repeat(inv, per_group)
    shift = norm_bias - jnp.repeat(mean, per_group) * scale
    normed = (source * scale + shift).astype(jnp.bfloat16)
    kernel = conv_weight.astype(jnp.float32).reshape(3, 3, 3, C, C)
    conv = lax.conv_general_dilated(normed.astype(jnp.float32)[None], kernel, (1, 1, 1), 'SAME', dimension_numbers=('NDHWC', 'DHWIO', 'NDHWC'), precision=lax.Precision.HIGHEST)
    hidden = jax.nn.silu(conv).astype(jnp.bfloat16)
    down_kernel = down_weight.astype(jnp.float32).reshape(2, 2, 2, C, C2)
    reduced = lax.conv_general_dilated(hidden.astype(jnp.float32), down_kernel, (2, 2, 2), 'VALID', dimension_numbers=('NDHWC', 'DHWIO', 'NDHWC'), precision=lax.Precision.HIGHEST)
    return reduced[0].astype(jnp.bfloat16)
```

```python
import functools

import jax
import jax.numpy as jnp
from jax import lax
from jax.experimental import pallas as pl
from jax.experimental.pallas import tpu as pltpu
from jax.sharding import PartitionSpec as P

GROUPS = 32
LANES = 128
ROWS = 8
NROWS = 2
MESH = pl.DeviceIdType.MESH


def kernel(
    count,
    vol_hbm, gain_ref, bias_ref, conv_hbm, down_hbm,
    out_ref,
    vol, low, high, conv_w, down_w, taps, acc, slots,
    vol_sem, w_sem, halo_send, halo_recv, stat_send, stat_recv,
):
    planes, height, width, chans = vol.shape
    me = lax.axis_index("sp")

    barrier = pltpu.get_barrier_semaphore()

    def greet(k, _):
        pl.semaphore_signal(
            barrier, inc=1, device_id={"sp": lax.rem(me + k, count)}, device_id_type=MESH
        )
        return 0

    lax.fori_loop(1, count, greet, 0)
    vol_copies = [
        pltpu.make_async_copy(vol_hbm.at[p], vol.at[p], vol_sem.at[p]) for p in range(planes)
    ]
    for copy in vol_copies:
        copy.start()
    conv_copy = pltpu.make_async_copy(conv_hbm, conv_w, w_sem.at[0])
    down_copy = pltpu.make_async_copy(down_hbm, down_w, w_sem.at[1])
    conv_copy.start()
    down_copy.start()
    pl.semaphore_wait(barrier, count - 1)

    up = pltpu.make_async_remote_copy(
        vol_hbm.at[planes - 1], low, halo_send.at[0], halo_recv.at[0],
        device_id={"sp": lax.rem(me + 1, count)}, device_id_type=MESH,
    )
    down = pltpu.make_async_remote_copy(
        vol_hbm.at[0], high, halo_send.at[1], halo_recv.at[1],
        device_id={"sp": lax.rem(me + count - 1, count)}, device_id_type=MESH,
    )

    @pl.when(me < count - 1)
    def _():
        up.start()

    @pl.when(me > 0)
    def _():
        down.start()

    srows = 2
    zero = jnp.zeros((8, chans), jnp.float32)
    sums = (zero, zero)
    for p in range(planes):
        vol_copies[p].wait()

        def add(i, carry, p=p):
            total, squares = carry
            block = vol[p, pl.ds(i * srows, srows)].astype(jnp.float32)
            block = block.reshape(srows * width // 8, 8, chans)
            return total + jnp.sum(block, axis=0), squares + jnp.sum(block * block, axis=0)

        sums = lax.fori_loop(0, height // srows, add, sums, unroll=4)
    row = lax.broadcasted_iota(jnp.int32, (8, chans), 0)
    slots[me] = jnp.where(
        row == 0,
        jnp.sum(sums[0], axis=0, keepdims=True),
        jnp.where(row == 1, jnp.sum(sums[1], axis=0, keepdims=True), 0.0),
    )

    def stat_copy(k):
        return pltpu.make_async_remote_copy(
            slots.at[me], slots.at[me], stat_send.at[k], stat_recv.at[me],
            device_id={"sp": lax.rem(me + k, count)}, device_id_type=MESH,
        )

    def send(k, _):
        stat_copy(k).start()
        return 0

    lax.fori_loop(1, count, send, 0)

    edge = jnp.zeros((planes + 2, 1, width, 3 * chans), jnp.bfloat16)
    taps[:, 0:1] = edge
    taps[:, height + 1 : height + 2] = edge

    def receive(k, _):
        source = lax.rem(me + k, count)
        pltpu.make_async_remote_copy(
            slots.at[source], slots.at[source], stat_send.at[k], stat_recv.at[source],
            device_id={"sp": source}, device_id_type=MESH,
        ).wait_recv()
        return 0

    lax.fori_loop(1, count, receive, 0)
    total = jnp.sum(slots[...], axis=0)
    per_group = chans // GROUPS
    lane = lax.broadcasted_iota(jnp.int32, (8, chans), 1)
    step = 1
    while step < per_group:
        other = jnp.where(
            (lane & step) == 0,
            pltpu.roll(total, chans - step, 1),
            pltpu.roll(total, step, 1),
        )
        total = total + other
        step *= 2
    cells = planes * count * height * width * per_group
    mean = total[0:1] * (1.0 / cells)
    var = total[1:2] * (1.0 / cells) - mean * mean
    scale = gain_ref[...] * lax.rsqrt(var + 1e-05)
    shift = bias_ref[...] - mean * scale

    nrow = lax.broadcasted_iota(jnp.int32, (NROWS * width, chans), 0)
    first = nrow == 0
    last = nrow == width - 1
    for r in range(1, NROWS):
        first = first | (nrow == r * width)
        last = last | (nrow == r * width + width - 1)

    def normalise(source, plane):
        def one(i, _):
            h = i * NROWS
            block = source[pl.ds(h, NROWS)].astype(jnp.float32)
            block = block.reshape(NROWS * width, chans) * scale + shift
            before = jnp.where(first, 0.0, pltpu.roll(block, 1, 0))
            after = jnp.where(last, 0.0, pltpu.roll(block, NROWS * width - 1, 0))
            for c, value in enumerate((before, block, after)):
                taps[plane, pl.ds(h + 1, NROWS), :, c * chans : (c + 1) * chans] = value.astype(
                    jnp.bfloat16
                ).reshape(NROWS, width, chans)
            return 0

        lax.fori_loop(0, height // NROWS, one, 0, unroll=2)

    for p in range(planes):
        normalise(vol.at[p], p + 1)
    conv_copy.wait()

    def window(plane, h):
        return jnp.concatenate(
            [
                taps[plane, pl.ds(h + b, ROWS)].reshape(ROWS * width, 3 * chans)
                for b in range(3)
            ],
            axis=1,
        )

    def weight(a):
        return conv_w[9 * a : 9 * a + 9].reshape(9 * chans, chans)

    def inner(i, _):
        h = i * ROWS
        lhs = [window(p + 1, h) for p in range(2)]
        for out in range(2):
            value = jnp.dot(lhs[0], weight(1 - out), preferred_element_type=jnp.float32)
            value += jnp.dot(lhs[1], weight(2 - out), preferred_element_type=jnp.float32)
            value = value.reshape(ROWS, width, chans)
            for part in range(chans // LANES):
                acc[part, out, pl.ds(h, ROWS)] = value[:, :, part * LANES : (part + 1) * LANES]
        return 0

    lax.fori_loop(0, height // ROWS, inner, 0)

    @pl.when(me > 0)
    def _():
        up.wait_recv()
        normalise(low, 0)

    @pl.when(me == 0)
    def _():
        taps[0] = jnp.zeros(taps.shape[1:], jnp.bfloat16)

    @pl.when(me < count - 1)
    def _():
        down.wait_recv()
        normalise(high, planes + 1)

    @pl.when(me == count - 1)
    def _():
        taps[planes + 1] = jnp.zeros(taps.shape[1:], jnp.bfloat16)

    def outer(i, _):
        h = i * ROWS
        for out in range(2):
            value = jnp.dot(
                window(3 * out, h), weight(2 * out), preferred_element_type=jnp.float32
            ).reshape(ROWS, width, chans)
            for part in range(chans // LANES):
                half = value[:, :, part * LANES : (part + 1) * LANES]
                half = 0.5 * (half + acc[part, out, pl.ds(h, ROWS)])
                acc[part, out, pl.ds(h, ROWS)] = half + half * jnp.tanh(half)
        return 0

    lax.fori_loop(0, height // ROWS, outer, 0)

    down_copy.wait()
    hidden = acc.reshape(chans // LANES, 2, height // 2, 2 * width, LANES)
    pieces = []
    for a in range(2):
        for b in range(2):
            for c in range(2):
                for part in range(chans // LANES):
                    piece = hidden[part, a, :, pl.ds(b * width + c, width // 2, stride=2), :]
                    pieces.append(
                        piece.reshape(height // 2 * (width // 2), LANES).astype(jnp.bfloat16)
                    )
    result = jnp.dot(
        jnp.concatenate(pieces, axis=1),
        down_w[...].reshape(8 * chans, down_w.shape[2]),
        preferred_element_type=jnp.float32,
    )
    out_ref[...] = result.astype(jnp.bfloat16).reshape(out_ref.shape)

    @pl.when(me < count - 1)
    def _():
        up.wait_send()

    @pl.when(me > 0)
    def _():
        down.wait_send()

    def sent(k, _):
        stat_copy(k).wait_send()
        return 0

    lax.fori_loop(1, count, sent, 0)


def body(volume, norm_gain, norm_bias, conv_weight, down_weight):
    planes, height, width, chans = volume.shape
    count = lax.axis_size("sp")
    chans2 = down_weight.shape[2]
    return pl.pallas_call(
        functools.partial(kernel, count),
        out_shape=jax.ShapeDtypeStruct((planes // 2, height // 2, width // 2, chans2), jnp.bfloat16),
        in_specs=[
            pl.BlockSpec(memory_space=pl.ANY),
            pl.BlockSpec(memory_space=pltpu.VMEM),
            pl.BlockSpec(memory_space=pltpu.VMEM),
            pl.BlockSpec(memory_space=pl.ANY),
            pl.BlockSpec(memory_space=pl.ANY),
        ],
        out_specs=pl.BlockSpec(memory_space=pltpu.VMEM),
        scratch_shapes=[
            pltpu.VMEM((planes, height, width, chans), jnp.bfloat16),
            pltpu.VMEM((height, width, chans), jnp.bfloat16),
            pltpu.VMEM((height, width, chans), jnp.bfloat16),
            pltpu.VMEM(conv_weight.shape, jnp.bfloat16),
            pltpu.VMEM(down_weight.shape, jnp.bfloat16),
            pltpu.VMEM((planes + 2, height + 2, width, 3 * chans), jnp.bfloat16),
            pltpu.VMEM((chans // LANES, 2, height, width, LANES), jnp.float32),
            pltpu.VMEM((count, 8, chans), jnp.float32),
            pltpu.SemaphoreType.DMA((planes,)),
            pltpu.SemaphoreType.DMA((2,)),
            pltpu.SemaphoreType.DMA((2,)),
            pltpu.SemaphoreType.DMA((2,)),
            pltpu.SemaphoreType.DMA((count,)),
            pltpu.SemaphoreType.DMA((count,)),
        ],
        compiler_params=pltpu.CompilerParams(
            collective_id=0, has_side_effects=True, vmem_limit_bytes=56 * 2**20
        ),
        name="encoder",
    )(volume, norm_gain.reshape(1, chans), norm_bias.reshape(1, chans), conv_weight, down_weight)


def solution(mesh):
    in_specs = (P(("grp", "sp"), None, None, None), P(), P(), P(), P())
    out_specs = P(("grp", "sp"), None, None, None)
    return jax.shard_map(body, mesh=mesh, in_specs=in_specs, out_specs=out_specs, check_vma=False)
```

```python
import functools

import jax
import jax.numpy as jnp
from jax import lax
from jax.experimental import pallas as pl
from jax.experimental.pallas import tpu as pltpu
from jax.sharding import PartitionSpec as P

GROUPS = 32
LANES = 128
ROWS = 8
CHUNK = 8
NROWS = 2
MESH = pl.DeviceIdType.MESH


def kernel(
    count,
    vol_hbm, gain_ref, bias_ref, conv_hbm, down_hbm,
    out_ref,
    vol, near, far, conv_w, down_w, taps, acc, slots,
    vol_sem, w_sem, near_sem, far_send, far_recv, stat_send, stat_recv,
):
    planes, height, width, chans = vol.shape
    me = lax.axis_index("sp")

    barrier = pltpu.get_barrier_semaphore()

    def greet(k, _):
        pl.semaphore_signal(
            barrier, inc=1, device_id={"sp": lax.rem(me + k, count)}, device_id_type=MESH
        )
        return 0

    lax.fori_loop(1, count, greet, 0)
    vol_copies = [
        pltpu.make_async_copy(vol_hbm.at[p], vol.at[p], vol_sem.at[p]) for p in range(planes)
    ]
    for copy in vol_copies:
        copy.start()
    conv_copy = pltpu.make_async_copy(conv_hbm, conv_w, w_sem.at[0])
    down_copy = pltpu.make_async_copy(down_hbm, down_w, w_sem.at[1])
    conv_copy.start()
    down_copy.start()
    pl.semaphore_wait(barrier, count - 1)

    odd = lax.rem(me, 2)
    even = 1 - odd
    has_far = jnp.logical_and(me > 0, me < count - 1)
    far_device = lax.rem(me + 2 * odd - 1 + count, count)
    near_copy = pltpu.make_async_remote_copy(
        vol_hbm.at[even], near, near_sem.at[0], near_sem.at[1],
        device_id={"sp": me + 1 - 2 * odd}, device_id_type=MESH,
    )
    far_copies = [
        pltpu.make_async_remote_copy(
            vol_hbm.at[odd, pl.ds(k * CHUNK, CHUNK)], far.at[pl.ds(k * CHUNK, CHUNK)],
            far_send.at[k], far_recv.at[k],
            device_id={"sp": far_device}, device_id_type=MESH,
        )
        for k in range(height // CHUNK)
    ]

    srows = 2
    zero = jnp.zeros((8, chans), jnp.float32)
    sums = (zero, zero)
    for p in range(planes):
        vol_copies[p].wait()

        def add(i, carry, p=p):
            total, squares = carry
            block = vol[p, pl.ds(i * srows, srows)].astype(jnp.float32)
            block = block.reshape(srows * width // 8, 8, chans)
            return total + jnp.sum(block, axis=0), squares + jnp.sum(block * block, axis=0)

        sums = lax.fori_loop(0, height // srows, add, sums, unroll=4)
    row = lax.broadcasted_iota(jnp.int32, (8, chans), 0)
    slots[me] = jnp.where(
        row == 0,
        jnp.sum(sums[0], axis=0, keepdims=True),
        jnp.where(row == 1, jnp.sum(sums[1], axis=0, keepdims=True), 0.0),
    )

    def stat_copy(k):
        return pltpu.make_async_remote_copy(
            slots.at[me], slots.at[me], stat_send.at[k], stat_recv.at[me],
            device_id={"sp": lax.rem(me + k, count)}, device_id_type=MESH,
        )

    def send(k, _):
        stat_copy(k).start()
        return 0

    lax.fori_loop(1, count, send, 0)

    near_copy.start()

    @pl.when(has_far)
    def _():
        for copy in far_copies:
            copy.start()

    edge = jnp.zeros((planes + 2, 1, width, 3 * chans), jnp.bfloat16)
    taps[:, 0:1] = edge
    taps[:, height + 1 : height + 2] = edge

    def receive(k, _):
        source = lax.rem(me + k, count)
        pltpu.make_async_remote_copy(
            slots.at[source], slots.at[source], stat_send.at[k], stat_recv.at[source],
            device_id={"sp": source}, device_id_type=MESH,
        ).wait_recv()
        return 0

    lax.fori_loop(1, count, receive, 0)
    total = jnp.sum(slots[...], axis=0)
    per_group = chans // GROUPS
    lane = lax.broadcasted_iota(jnp.int32, (8, chans), 1)
    step = 1
    while step < per_group:
        other = jnp.where(
            (lane & step) == 0,
            pltpu.roll(total, chans - step, 1),
            pltpu.roll(total, step, 1),
        )
        total = total + other
        step *= 2
    cells = planes * count * height * width * per_group
    mean = total[0:1] * (1.0 / cells)
    var = total[1:2] * (1.0 / cells) - mean * mean
    scale = gain_ref[...] * lax.rsqrt(var + 1e-05)
    shift = bias_ref[...] - mean * scale

    nrow = lax.broadcasted_iota(jnp.int32, (NROWS * width, chans), 0)
    first = nrow == 0
    last = nrow == width - 1
    for r in range(1, NROWS):
        first = first | (nrow == r * width)
        last = last | (nrow == r * width + width - 1)

    def normalise(source, plane, start, stop):
        def one(i, _):
            h = i * NROWS
            block = source[pl.ds(h, NROWS)].astype(jnp.float32)
            block = block.reshape(NROWS * width, chans) * scale + shift
            before = jnp.where(first, 0.0, pltpu.roll(block, 1, 0))
            after = jnp.where(last, 0.0, pltpu.roll(block, NROWS * width - 1, 0))
            for c, value in enumerate((before, block, after)):
                taps[plane, pl.ds(h + 1, NROWS), :, c * chans : (c + 1) * chans] = value.astype(
                    jnp.bfloat16
                ).reshape(NROWS, width, chans)
            return 0

        lax.fori_loop(start // NROWS, stop // NROWS, one, 0, unroll=2)

    for p in range(planes):
        normalise(vol.at[p], p + 1, 0, height)
    conv_copy.wait()

    def window(plane, h, rows):
        return jnp.concatenate(
            [
                taps[plane, pl.ds(h + b, rows)].reshape(rows * width, 3 * chans)
                for b in range(3)
            ],
            axis=1,
        )

    def weight(a):
        return conv_w[pl.ds(9 * a, 9)].reshape(9 * chans, chans)

    def inner(i, _):
        h = i * ROWS
        lhs = [window(p + 1, h, ROWS) for p in range(2)]
        for out in range(2):
            value = jnp.dot(lhs[0], weight(1 - out), preferred_element_type=jnp.float32)
            value += jnp.dot(lhs[1], weight(2 - out), preferred_element_type=jnp.float32)
            value = value.reshape(ROWS, width, chans)
            for part in range(chans // LANES):
                acc[part, out, pl.ds(h, ROWS)] = value[:, :, part * LANES : (part + 1) * LANES]
        return 0

    lax.fori_loop(0, height // ROWS, inner, 0)

    def finish(out, h, rows):
        value = jnp.dot(
            window(3 * out, h, rows), weight(2 * out), preferred_element_type=jnp.float32
        ).reshape(rows, width, chans)
        for part in range(chans // LANES):
            half = value[:, :, part * LANES : (part + 1) * LANES]
            half = 0.5 * (half + acc[part, out, pl.ds(h, rows)])
            acc[part, out, pl.ds(h, rows)] = half + half * jnp.tanh(half)

    near_copy.wait_recv()
    normalise(near, 3 * even, 0, height)

    def outer(i, _):
        finish(even, i * ROWS, ROWS)
        return 0

    lax.fori_loop(0, height // ROWS, outer, 0)

    @pl.when(jnp.logical_not(has_far))
    def _():
        taps[3 * odd] = jnp.zeros(taps.shape[1:], jnp.bfloat16)

    done = 0
    for k, copy in enumerate(far_copies):
        ready = (k + 1) * CHUNK

        @pl.when(has_far)
        def _():
            copy.wait_recv()
            normalise(far, 3 * odd, k * CHUNK, ready)

        until = height if ready == height else ready - 1
        finish(odd, done, until - done)
        done = until

    down_copy.wait()
    hidden = acc.reshape(chans // LANES, 2, height // 2, 2 * width, LANES)
    pieces = []
    for a in range(2):
        for b in range(2):
            for c in range(2):
                for part in range(chans // LANES):
                    piece = hidden[part, a, :, pl.ds(b * width + c, width // 2, stride=2), :]
                    pieces.append(
                        piece.reshape(height // 2 * (width // 2), LANES).astype(jnp.bfloat16)
                    )
    result = jnp.dot(
        jnp.concatenate(pieces, axis=1),
        down_w[...].reshape(8 * chans, down_w.shape[2]),
        preferred_element_type=jnp.float32,
    )
    out_ref[...] = result.astype(jnp.bfloat16).reshape(out_ref.shape)

    near_copy.wait_send()

    @pl.when(has_far)
    def _():
        for copy in far_copies:
            copy.wait_send()

    def sent(k, _):
        stat_copy(k).wait_send()
        return 0

    lax.fori_loop(1, count, sent, 0)


def body(volume, norm_gain, norm_bias, conv_weight, down_weight):
    planes, height, width, chans = volume.shape
    count = lax.axis_size("sp")
    chans2 = down_weight.shape[2]
    return pl.pallas_call(
        functools.partial(kernel, count),
        out_shape=jax.ShapeDtypeStruct((planes // 2, height // 2, width // 2, chans2), jnp.bfloat16),
        in_specs=[
            pl.BlockSpec(memory_space=pl.ANY),
            pl.BlockSpec(memory_space=pltpu.VMEM),
            pl.BlockSpec(memory_space=pltpu.VMEM),
            pl.BlockSpec(memory_space=pl.ANY),
            pl.BlockSpec(memory_space=pl.ANY),
        ],
        out_specs=pl.BlockSpec(memory_space=pltpu.VMEM),
        scratch_shapes=[
            pltpu.VMEM((planes, height, width, chans), jnp.bfloat16),
            pltpu.VMEM((height, width, chans), jnp.bfloat16),
            pltpu.VMEM((height, width, chans), jnp.bfloat16),
            pltpu.VMEM(conv_weight.shape, jnp.bfloat16),
            pltpu.VMEM(down_weight.shape, jnp.bfloat16),
            pltpu.VMEM((planes + 2, height + 2, width, 3 * chans), jnp.bfloat16),
            pltpu.VMEM((chans // LANES, 2, height, width, LANES), jnp.float32),
            pltpu.VMEM((count, 8, chans), jnp.float32),
            pltpu.SemaphoreType.DMA((planes,)),
            pltpu.SemaphoreType.DMA((2,)),
            pltpu.SemaphoreType.DMA((2,)),
            pltpu.SemaphoreType.DMA((height // CHUNK,)),
            pltpu.SemaphoreType.DMA((height // CHUNK,)),
            pltpu.SemaphoreType.DMA((count,)),
            pltpu.SemaphoreType.DMA((count,)),
        ],
        compiler_params=pltpu.CompilerParams(
            collective_id=0, has_side_effects=True, vmem_limit_bytes=56 * 2**20
        ),
        name="encoder",
    )(volume, norm_gain.reshape(1, chans), norm_bias.reshape(1, chans), conv_weight, down_weight)


def solution(mesh):
    in_specs = (P(("grp", "sp"), None, None, None), P(), P(), P(), P())
    out_specs = P(("grp", "sp"), None, None, None)
    return jax.shard_map(body, mesh=mesh, in_specs=in_specs, out_specs=out_specs, check_vma=False)
```

```python
import functools

import jax
import jax.numpy as jnp
from jax import lax
from jax.experimental import pallas as pl
from jax.experimental.pallas import tpu as pltpu
from jax.sharding import PartitionSpec as P

GROUPS = 32
LANES = 128
ROWS = 16
CHUNK = 8
NROWS = 2
MESH = pl.DeviceIdType.MESH


def kernel(
    count,
    vol_hbm, gain_ref, bias_ref, conv_hbm, down_hbm,
    out_ref,
    vol, near, far, conv_w, down_w, taps, acc, slots,
    vol_sem, w_sem, near_sem, far_send, far_recv, stat_send, stat_recv,
):
    planes, height, width, chans = vol.shape
    me = lax.axis_index("sp")

    barrier = pltpu.get_barrier_semaphore()

    def greet(k, _):
        pl.semaphore_signal(
            barrier, inc=1, device_id={"sp": lax.rem(me + k, count)}, device_id_type=MESH
        )
        return 0

    lax.fori_loop(1, count, greet, 0)
    vol_copies = [
        pltpu.make_async_copy(vol_hbm.at[p], vol.at[p], vol_sem.at[p]) for p in range(planes)
    ]
    for copy in vol_copies:
        copy.start()
    conv_copy = pltpu.make_async_copy(conv_hbm, conv_w, w_sem.at[0])
    down_copy = pltpu.make_async_copy(down_hbm, down_w, w_sem.at[1])
    conv_copy.start()
    down_copy.start()

    odd = lax.rem(me, 2)
    even = 1 - odd
    has_far = jnp.logical_and(me > 0, me < count - 1)
    far_device = lax.rem(me + 2 * odd - 1 + count, count)
    near_copy = pltpu.make_async_remote_copy(
        vol_hbm.at[even], near, near_sem.at[0], near_sem.at[1],
        device_id={"sp": me + 1 - 2 * odd}, device_id_type=MESH,
    )
    far_copies = [
        pltpu.make_async_remote_copy(
            vol_hbm.at[odd, pl.ds(k * CHUNK, CHUNK)], far.at[pl.ds(k * CHUNK, CHUNK)],
            far_send.at[k], far_recv.at[k],
            device_id={"sp": far_device}, device_id_type=MESH,
        )
        for k in range(height // CHUNK)
    ]

    srows = 2
    zero = jnp.zeros((8, chans), jnp.float32)
    sums = (zero, zero)
    for p in range(planes):
        vol_copies[p].wait()

        def add(i, carry, p=p):
            total, squares = carry
            block = vol[p, pl.ds(i * srows, srows)].astype(jnp.float32)
            block = block.reshape(srows * width // 8, 8, chans)
            return total + jnp.sum(block, axis=0), squares + jnp.sum(block * block, axis=0)

        sums = lax.fori_loop(0, height // srows, add, sums, unroll=4)
    row = lax.broadcasted_iota(jnp.int32, (8, chans), 0)
    slots[me] = jnp.where(
        row == 0,
        jnp.sum(sums[0], axis=0, keepdims=True),
        jnp.where(row == 1, jnp.sum(sums[1], axis=0, keepdims=True), 0.0),
    )

    def stat_copy(k):
        return pltpu.make_async_remote_copy(
            slots.at[me], slots.at[me], stat_send.at[k], stat_recv.at[me],
            device_id={"sp": lax.rem(me + k, count)}, device_id_type=MESH,
        )

    def send(k, _):
        stat_copy(k).start()
        return 0

    pl.semaphore_wait(barrier, count - 1)
    lax.fori_loop(1, count, send, 0)

    near_copy.start()

    @pl.when(has_far)
    def _():
        for copy in far_copies:
            copy.start()

    edge = jnp.zeros((planes + 2, 1, width, 3 * chans), jnp.bfloat16)
    taps[:, 0:1] = edge
    taps[:, height + 1 : height + 2] = edge

    def receive(k, _):
        source = lax.rem(me + k, count)
        pltpu.make_async_remote_copy(
            slots.at[source], slots.at[source], stat_send.at[k], stat_recv.at[source],
            device_id={"sp": source}, device_id_type=MESH,
        ).wait_recv()
        return 0

    lax.fori_loop(1, count, receive, 0)
    total = jnp.sum(slots[...], axis=0)
    per_group = chans // GROUPS
    lane = lax.broadcasted_iota(jnp.int32, (8, chans), 1)
    step = 1
    while step < per_group:
        other = jnp.where(
            (lane & step) == 0,
            pltpu.roll(total, chans - step, 1),
            pltpu.roll(total, step, 1),
        )
        total = total + other
        step *= 2
    cells = planes * count * height * width * per_group
    mean = total[0:1] * (1.0 / cells)
    var = total[1:2] * (1.0 / cells) - mean * mean
    scale = gain_ref[...] * lax.rsqrt(var + 1e-05)
    shift = bias_ref[...] - mean * scale

    nrow = lax.broadcasted_iota(jnp.int32, (NROWS * width, chans), 0)
    first = nrow == 0
    last = nrow == width - 1
    for r in range(1, NROWS):
        first = first | (nrow == r * width)
        last = last | (nrow == r * width + width - 1)

    def normalise_rows(source, plane, h):
        block = source[pl.ds(h, NROWS)].astype(jnp.float32)
        block = block.reshape(NROWS * width, chans) * scale + shift
        before = jnp.where(first, 0.0, pltpu.roll(block, 1, 0))
        after = jnp.where(last, 0.0, pltpu.roll(block, NROWS * width - 1, 0))
        for c, value in enumerate((before, block, after)):
            taps[plane, pl.ds(h + 1, NROWS), :, c * chans : (c + 1) * chans] = value.astype(
                jnp.bfloat16
            ).reshape(NROWS, width, chans)

    def normalise(source, plane, start, stop):
        def one(i, _):
            normalise_rows(source, plane, i * NROWS)
            return 0

        lax.fori_loop(start // NROWS, stop // NROWS, one, 0, unroll=2)

    conv_copy.wait()

    def window(plane, h, rows):
        return jnp.concatenate(
            [
                taps[plane, pl.ds(h + b, rows)].reshape(rows * width, 3 * chans)
                for b in range(3)
            ],
            axis=1,
        )

    def weight(a):
        return conv_w[pl.ds(9 * a, 9)].reshape(9 * chans, chans)

    def inner(h, rows):
        lhs = [window(p + 1, h, rows) for p in range(2)]
        for out in range(2):
            value = jnp.dot(lhs[0], weight(1 - out), preferred_element_type=jnp.float32)
            value += jnp.dot(lhs[1], weight(2 - out), preferred_element_type=jnp.float32)
            value = value.reshape(rows, width, chans)
            for part in range(chans // LANES):
                acc[part, out, pl.ds(h, rows)] = value[:, :, part * LANES : (part + 1) * LANES]

    ahead = (8, 16, 24, height)
    for p in range(planes):
        normalise(vol.at[p], p + 1, 0, ahead[0])
    done = 0
    for k, ready in enumerate(ahead):
        if ready < height:
            for p in range(planes):
                for h in range(ready, ahead[k + 1], NROWS):
                    normalise_rows(vol.at[p], p + 1, h)
        until = height if ready == height else ready - 1
        inner(done, until - done)
        done = until

    def finish(out, h, rows):
        value = jnp.dot(
            window(3 * out, h, rows), weight(2 * out), preferred_element_type=jnp.float32
        ).reshape(rows, width, chans)
        for part in range(chans // LANES):
            half = value[:, :, part * LANES : (part + 1) * LANES]
            half = 0.5 * (half + acc[part, out, pl.ds(h, rows)])
            acc[part, out, pl.ds(h, rows)] = half + half * jnp.tanh(half)

    near_copy.wait_recv()
    normalise(near, 3 * even, 0, height)

    def outer(i, _):
        finish(even, i * ROWS, ROWS)
        return 0

    lax.fori_loop(0, height // ROWS, outer, 0)

    @pl.when(jnp.logical_not(has_far))
    def _():
        taps[3 * odd] = jnp.zeros(taps.shape[1:], jnp.bfloat16)

    done = 0
    for k, copy in enumerate(far_copies):
        ready = (k + 1) * CHUNK

        @pl.when(has_far)
        def _():
            copy.wait_recv()
            normalise(far, 3 * odd, k * CHUNK, ready)

        until = height if ready == height else ready - 1
        finish(odd, done, until - done)
        done = until

    down_copy.wait()
    hidden = acc.reshape(chans // LANES, 2, height // 2, 2 * width, LANES)
    pieces = []
    for a in range(2):
        for b in range(2):
            for c in range(2):
                for part in range(chans // LANES):
                    piece = hidden[part, a, :, pl.ds(b * width + c, width // 2, stride=2), :]
                    pieces.append(
                        piece.reshape(height // 2 * (width // 2), LANES).astype(jnp.bfloat16)
                    )
    result = jnp.dot(
        jnp.concatenate(pieces, axis=1),
        down_w[...].reshape(8 * chans, down_w.shape[2]),
        preferred_element_type=jnp.float32,
    )
    out_ref[...] = result.astype(jnp.bfloat16).reshape(out_ref.shape)

    near_copy.wait_send()

    @pl.when(has_far)
    def _():
        for copy in far_copies:
            copy.wait_send()

    def sent(k, _):
        stat_copy(k).wait_send()
        return 0

    lax.fori_loop(1, count, sent, 0)


def body(volume, norm_gain, norm_bias, conv_weight, down_weight):
    planes, height, width, chans = volume.shape
    count = lax.axis_size("sp")
    chans2 = down_weight.shape[2]
    return pl.pallas_call(
        functools.partial(kernel, count),
        out_shape=jax.ShapeDtypeStruct((planes // 2, height // 2, width // 2, chans2), jnp.bfloat16),
        in_specs=[
            pl.BlockSpec(memory_space=pl.ANY),
            pl.BlockSpec(memory_space=pltpu.VMEM),
            pl.BlockSpec(memory_space=pltpu.VMEM),
            pl.BlockSpec(memory_space=pl.ANY),
            pl.BlockSpec(memory_space=pl.ANY),
        ],
        out_specs=pl.BlockSpec(memory_space=pltpu.VMEM),
        scratch_shapes=[
            pltpu.VMEM((planes, height, width, chans), jnp.bfloat16),
            pltpu.VMEM((height, width, chans), jnp.bfloat16),
            pltpu.VMEM((height, width, chans), jnp.bfloat16),
            pltpu.VMEM(conv_weight.shape, jnp.bfloat16),
            pltpu.VMEM(down_weight.shape, jnp.bfloat16),
            pltpu.VMEM((planes + 2, height + 2, width, 3 * chans), jnp.bfloat16),
            pltpu.VMEM((chans // LANES, 2, height, width, LANES), jnp.float32),
            pltpu.VMEM((count, 8, chans), jnp.float32),
            pltpu.SemaphoreType.DMA((planes,)),
            pltpu.SemaphoreType.DMA((2,)),
            pltpu.SemaphoreType.DMA((2,)),
            pltpu.SemaphoreType.DMA((height // CHUNK,)),
            pltpu.SemaphoreType.DMA((height // CHUNK,)),
            pltpu.SemaphoreType.DMA((count,)),
            pltpu.SemaphoreType.DMA((count,)),
        ],
        compiler_params=pltpu.CompilerParams(
            collective_id=0, has_side_effects=True, vmem_limit_bytes=56 * 2**20
        ),
        name="encoder",
    )(volume, norm_gain.reshape(1, chans), norm_bias.reshape(1, chans), conv_weight, down_weight)


def solution(mesh):
    in_specs = (P(("grp", "sp"), None, None, None), P(), P(), P(), P())
    out_specs = P(("grp", "sp"), None, None, None)
    return jax.shard_map(body, mesh=mesh, in_specs=in_specs, out_specs=out_specs, check_vma=False)
```
